32 devices in a mesh: row: 4 (over x, core), col: 8 (over z, y).
Axes of the slice: x: 2, y: 2, z: 4, core: 2. Of those that a mesh axis runs over, the one named last changes fastest.
Arguments:
- residual: bfloat16 [30720, 512], P('row', 'col'), may hold values from -4 to 4
- interaction: bfloat16 [30720, 5120], P('row', 'col'), may hold values from -0.078125 to 0.078125
- commands: bfloat16 [5120, 512], P('col'), may hold values from -6 to 6
- slope_valid: int32 [240], P('row'), may hold values 0 or 1
- frame_valid: int32 [512], P('col'), may hold values 0 or 1
Outputs:
- covariance: bfloat16 [30720, 30720], P('row', 'col')
The draws below stay inside these ranges and needn't reach their ends.
All inputs are finite; a program needn't handle non-finite values. No bound on the sum of `slope_valid` or of `frame_valid` on one device may be relied on, other than what follows from the above.
Results may differ from the reference program's by a relative error of at most 0.02.
Values may be sent and summed in bfloat16 or wider, within the bound.
A program may use at most 128 MiB of HBM per device.

```python
import jax
import jax.numpy as jnp
from jax import lax

NS = 30720
NA = 5120
SBLK = 128
FRAMES = 512
NSB = 240
N_ROW = 4
N_COL = 8


def touch_ends(values, stream_key, least, high):
    longest = values.shape.index(max(values.shape))
    spots = []
    for shift in (0, 1):
        where = [jax.random.randint(jax.random.fold_in(stream_key, axis), (), 0, length) for axis, length in enumerate(values.shape)]
        where[longest] = (where[longest] + shift) % values.shape[longest]
        spots.append(tuple(where))
    return values.at[spots[0]].set(least).at[spots[1]].set(high)


def steps_of(stream_key, extent, shards, least, largest):
    loudness = 1.0
    for axis_at, parts in shards:
        steps = jax.random.uniform(jax.random.fold_in(jax.random.fold_in(stream_key, 6), axis_at), (parts,), jnp.float32, least / len(shards), largest / len(shards))
        loudness = loudness * jnp.repeat(jnp.exp(steps), extent[axis_at] // parts).reshape((-1,) + (1,) * (len(extent) - 1 - axis_at))
    return loudness


def normal_values(rng, extent, scale, reach, pieces=(), held_as=jnp.bfloat16):
    result = jax.random.normal(rng, extent, jnp.float32) * scale
    if len(pieces) > 0:
        result = steps_of(rng, extent, pieces, -0.22, 0.18) * result
    return jnp.clip(result, min=-reach, max=reach).astype(held_as)


def setup_inputs(seed: int = 0) -> dict:
    arg_keys = jax.random.split(jax.random.key(seed), 6)
    residual = normal_values(arg_keys[0], (NS, FRAMES), 0.5, 4.0, ((0, 4), (1, 8)))
    interaction = normal_values(arg_keys[1], (NS, NA), NA ** -0.5, 0.078125, ((0, 4), (1, 8)))
    commands = normal_values(arg_keys[2], (NA, FRAMES), 1.0, 6.0, ((0, 8),))
    slope_valid = touch_ends((jax.random.randint(arg_keys[3], (NSB,), 0, 8) < 7).astype(jnp.int32), jax.random.fold_in(arg_keys[3], 1), 0, 1)
    frame_valid = touch_ends((jax.random.randint(arg_keys[4], (FRAMES,), 0, 8) < 7).astype(jnp.int32), jax.random.fold_in(arg_keys[4], 1), 0, 1)
    return dict(residual=residual, interaction=interaction, commands=commands, slope_valid=slope_valid, frame_valid=frame_valid)


def reference(residual, interaction, commands, slope_valid, frame_valid):
    width = NA // N_COL
    total = residual.astype(jnp.float32)
    for block in range(N_COL):
        term = jnp.dot(interaction[:, block * width:(block + 1) * width], commands[block * width:(block + 1) * width, :], preferred_element_type=jnp.float32)
        rounded = lax.optimization_barrier(term.astype(jnp.bfloat16))
        total = total + rounded.astype(jnp.float32)
    row_mask = (slope_valid[:, None] * jnp.ones((1, SBLK), jnp.int32)).reshape(-1).astype(jnp.float32)
    slopes = (total * row_mask[:, None] * frame_valid[None, :].astype(jnp.float32)).astype(jnp.bfloat16)
    block_rows = NS // N_ROW
    blocks = slopes.reshape(N_ROW, block_rows, FRAMES)
    starts = jnp.arange(N_ROW, dtype=jnp.int32) * block_rows

    def one_block(inputs):
        chosen, start = inputs
        tile = jnp.dot(chosen, slopes.T, preferred_element_type=jnp.float32) / FRAMES
        row_ids = start + jnp.arange(block_rows, dtype=jnp.int32)[:, None]
        col_ids = jnp.arange(NS, dtype=jnp.int32)[None, :]
        return jnp.where(row_ids <= col_ids, tile, jnp.float32(0.0)).astype(jnp.bfloat16)

    return lax.map(one_block, (blocks, starts)).reshape(NS, NS)
```

```python
import functools

import jax
import jax.numpy as jnp
from jax import lax
from jax.experimental import pallas as pl
from jax.experimental.pallas import tpu as pltpu
from jax.sharding import PartitionSpec as P

SBLK = 128
MESH = pl.DeviceIdType.MESH
LANES = 4


def divisor(n, limit, unit):
    best = n
    for d in range(unit, min(n, limit) + 1, unit):
        if n % d == 0:
            best = d
    return best


def ring_position(c, n):
    return lax.rem(c + 1, 2) * (c // 2) + lax.rem(c, 2) * (n - 1 - c // 2)


def ring_column(p, n):
    up = 2 * p
    down = 2 * (n - 1 - p) + 1
    return jnp.where(p < n // 2, up, down)


def comm_kernel(
    C, R, rows, fl, inter_hbm, resid_hbm, cmd_ref, sel_ref, rmask_ref, fmask_ref,
    s_hbm, col_hbm,
    inter, resid, stage, recv, own, fall,
    in_sem, rs_send, rs_recv, ag_send, ag_recv, m_send, m_recv, c_send, c_recv, own_sem,
):
    r = lax.axis_index("row")
    c = lax.axis_index("col")
    p = ring_position(c, C)
    nxt = ring_column(lax.rem(p + 1, C), C)
    prv = ring_column(lax.rem(p + C - 1, C), C)
    br = C * rows
    bc = br * R // C
    per_row = br // bc
    rc = c // per_row
    k0 = lax.rem(c, per_row) * (bc // rows)
    nk = bc // rows
    tile = divisor(rows, 256, 16)

    def load(k):
        return (
            pltpu.make_async_copy(inter_hbm.at[k], inter.at[k], in_sem.at[0, k]),
            pltpu.make_async_copy(resid_hbm.at[k], resid.at[k], in_sem.at[1, k]),
        )

    def start_load(k):
        for cp in load(k):
            cp.start()

    def wait_load(k):
        for cp in load(k):
            cp.wait()

    for i in range(1, C // 2):
        start_load(lax.rem(p + C - i, C))
        start_load(lax.rem(p + i, C))
    start_load(lax.rem(p + C // 2, C))
    start_load(p)

    barrier = pltpu.get_barrier_semaphore()
    for j in range(1, C):
        pl.semaphore_signal(
            barrier, inc=1, device_id=(r, lax.rem(c + j, C)), device_id_type=MESH
        )
    for j in range(1, R):
        pl.semaphore_signal(
            barrier, inc=1, device_id=(lax.rem(r + j, R), c), device_id_type=MESH
        )
    pl.semaphore_wait(barrier, C - 1 + R - 1)

    def mask_copy(j):
        return pltpu.make_async_remote_copy(
            src_ref=fmask_ref, dst_ref=fall.at[j - 1],
            send_sem=m_send.at[j - 1], recv_sem=m_recv.at[j - 1],
            device_id=(r, lax.rem(c + j, C)), device_id_type=MESH,
        )

    for j in range(1, C):
        mask_copy(j).start()

    def lane_is_up(l):
        return l < LANES // 2

    def rs_chunk(l, s):
        if lane_is_up(l):
            return lax.rem(p + 2 * C - 1 - s, C)
        return lax.rem(p + 1 + s, C)

    def ag_chunk(l, s):
        if lane_is_up(l):
            return lax.rem(p + 2 * C - s, C)
        return lax.rem(p + s, C)

    def rs_copy(l, s):
        return pltpu.make_async_remote_copy(
            src_ref=stage.at[l, s], dst_ref=recv.at[l, s],
            send_sem=rs_send.at[l, s], recv_sem=rs_recv.at[l, s],
            device_id=(r, nxt if lane_is_up(l) else prv), device_id_type=MESH,
        )

    def partial(l, k, t):
        at = pl.ds(pl.multiple_of(t * tile, 8), tile)
        cols = slice(l * fl, (l + 1) * fl)
        return jnp.dot(
            inter[k, at, :], cmd_ref[:, cols], preferred_element_type=jnp.float32
        ) + jnp.dot(
            resid[k, at, :], sel_ref[:, cols], preferred_element_type=jnp.float32
        )

    def rs_step(s, first):
        for l in range(LANES):
            k = rs_chunk(l, s)
            if not first:
                rs_copy(l, s - 1).wait_recv()

            def one(t, _, l=l, k=k):
                at = pl.ds(pl.multiple_of(t * tile, 8), tile)
                value = partial(l, k, t)
                if not first:
                    value = value + recv[l, s - 1, at, :].astype(jnp.float32)
                stage[l, s, at, :] = value.astype(jnp.bfloat16)
                return 0

            lax.fori_loop(0, rows // tile, one, 0)
            rs_copy(l, s).start()

    for s in range(C - 1):
        i = s + 1
        if i < C // 2:
            wait_load(lax.rem(p + C - i, C))
            wait_load(lax.rem(p + i, C))
        elif i == C // 2:
            wait_load(lax.rem(p + C // 2, C))
            wait_load(p)
        if s <= C // 2:
            rs_step(s, s == 0)
    if C - 1 > C // 2 + 1:
        lax.fori_loop(C // 2 + 1, C - 1, lambda s, _: (rs_step(s, False), 0)[1], 0)

    for j in range(1, C):
        mask_copy(j).wait_recv()
    frames = fmask_ref[...]
    for j in range(1, C):
        frames = frames + fall[j - 1]

    def ag_copy(l, s, from_own=False):
        k = ag_chunk(l, s)
        return pltpu.make_async_remote_copy(
            src_ref=own.at[l] if from_own else s_hbm.at[l, k],
            dst_ref=s_hbm.at[l, k],
            send_sem=ag_send.at[l, s], recv_sem=ag_recv.at[l, s],
            device_id=(r, nxt if lane_is_up(l) else prv), device_id_type=MESH,
        )

    def own_copy(l):
        return pltpu.make_async_copy(own.at[l], s_hbm.at[l, p], own_sem.at[l])

    for l in range(LANES):
        rs_copy(l, C - 2).wait_recv()

        def last(t, _, l=l):
            at = pl.ds(pl.multiple_of(t * tile, 8), tile)
            value = partial(l, p, t) + recv[l, C - 2, at, :].astype(jnp.float32)
            value = value * rmask_ref[p, at, :] * frames[0:1, l * fl:(l + 1) * fl]
            own[l, at, :] = value.astype(jnp.bfloat16)
            return 0

        lax.fori_loop(0, rows // tile, last, 0)
        ag_copy(l, 0, True).start()
        own_copy(l).start()

    def down(l, k):
        return pltpu.make_async_remote_copy(
            src_ref=col_hbm.at[l, k - k0], dst_ref=col_hbm.at[l, k - k0],
            send_sem=c_send.at[l, k - k0], recv_sem=c_recv.at[l, k - k0],
            device_id=(lax.rem(r + R - 1, R), c), device_id_type=MESH,
        )

    def down_first(l, k):
        return pltpu.make_async_remote_copy(
            src_ref=s_hbm.at[l, k], dst_ref=col_hbm.at[l, k - k0],
            send_sem=c_send.at[l, k - k0], recv_sem=c_recv.at[l, k - k0],
            device_id=(lax.rem(r + R - 1, R), c), device_id_type=MESH,
        )

    def chain(u):
        t = u - (rc - r)
        for l in range(LANES):
            if lane_is_up(l):
                k = lax.rem(p + 4 * C * R - t, C)
            else:
                k = lax.rem(p + 4 * C * R + t, C)
            live = (t >= 0) & (t < C) & (r <= rc) & (k >= k0) & (k < k0 + nk)

            @pl.when(live & (r < rc))
            def _(l=l, k=k):
                down(l, k).wait_recv()

            @pl.when(live & (r > 0) & (r < rc))
            def _(l=l, k=k):
                down(l, k).start()

            @pl.when(live & (r > 0) & (r == rc))
            def _(l=l, k=k):
                down_first(l, k).start()

    for l in range(LANES):
        own_copy(l).wait()
    chain(0)

    def ag_step(s, _):
        for l in range(LANES):
            ag_copy(l, s - 1).wait_recv()
            ag_copy(l, s).start()
        chain(s)
        return 0

    lax.fori_loop(1, C - 1, ag_step, 0)
    for l in range(LANES):
        ag_copy(l, C - 2).wait_recv()

    lax.fori_loop(C - 1, C + R - 1, lambda u, _: (chain(u), 0)[1], 0)

    def drain(s, _):
        for l in range(LANES):
            rs_copy(l, s).wait_send()
            ag_copy(l, s).wait_send()
        return 0

    lax.fori_loop(0, C - 1, drain, 0)
    for j in range(1, C):
        mask_copy(j).wait_send()

    def drain_down(i, _):
        for l in range(LANES):
            @pl.when((r > 0) & (r <= rc))
            def _(l=l):
                down(l, k0 + i).wait_send()
        return 0

    lax.fori_loop(0, nk, drain_down, 0)


def cov_kernel(C, R, br, bc, F, tm, tn, rows_ref, s_hbm, col_hbm, out_ref, cols, sem):
    r = lax.axis_index("row")
    c = lax.axis_index("col")
    i = pl.program_id(0)
    per_row = br // bc
    rc = c // per_row
    fl = F // LANES

    @pl.when(i == 0)
    def _():
        def copies(src):
            return [
                pltpu.make_async_copy(
                    src(l), cols.at[:, pl.ds(l * fl, fl)], sem.at[l]
                )
                for l in range(LANES)
            ]

        start = lax.rem(c, per_row) * bc

        @pl.when(r == rc)
        def _():
            cps = copies(lambda l: s_hbm.at[l, pl.ds(pl.multiple_of(start, 8), bc), :])
            for cp in cps:
                cp.start()
            for cp in cps:
                cp.wait()

        @pl.when(r < rc)
        def _():
            cps = copies(lambda l: col_hbm.at[l])
            for cp in cps:
                cp.start()
            for cp in cps:
                cp.wait()

    row0 = r * br + i * tm
    for j in range(bc // tn):
        col0 = c * bc + j * tn
        at = slice(j * tn, (j + 1) * tn)

        @pl.when(row0 >= col0 + tn)
        def _(at=at):
            out_ref[:, at] = jnp.zeros((tm, tn), jnp.bfloat16)

        def value(at=at):
            a = jnp.concatenate([rows_ref[l] for l in range(LANES)], axis=1)
            return lax.dot_general(
                a, cols[at, :], (((1,), (1,)), ((), ())),
                preferred_element_type=jnp.float32,
            ) / F

        @pl.when(row0 + tm <= col0)
        def _(at=at, value=value):
            out_ref[:, at] = value().astype(jnp.bfloat16)

        @pl.when((row0 < col0 + tn) & (row0 + tm > col0))
        def _(at=at, value=value, col0=col0):
            rid = row0 + lax.broadcasted_iota(jnp.int32, (tm, tn), 0)
            cid = col0 + lax.broadcasted_iota(jnp.int32, (tm, tn), 1)
            out_ref[:, at] = jnp.where(rid <= cid, value(), 0.0).astype(jnp.bfloat16)


def per_device(R, C, residual, interaction, commands, slope_valid, frame_valid):
    br, kd = interaction.shape
    F = commands.shape[1]
    fc = residual.shape[1]
    rows = br // C
    fl = F // LANES
    bc = br * R // C
    c = lax.axis_index("col")
    own_col = (
        c * fc + jnp.arange(fc, dtype=jnp.int32)[:, None]
        == jnp.arange(F, dtype=jnp.int32)[None, :]
    )
    sel = own_col.astype(jnp.bfloat16)
    fmask = jnp.sum(
        jnp.where(own_col, frame_valid[:, None], 0), axis=0, dtype=jnp.int32
    ).astype(jnp.float32)
    fmask = jnp.broadcast_to(fmask[None, :], (8, F))
    rmask = jnp.broadcast_to(slope_valid.astype(jnp.float32)[:, None], (br // SBLK, SBLK))
    rmask = rmask.reshape(C, rows, 1)
    any_spec = pl.BlockSpec(memory_space=pl.ANY)
    vmem = pl.BlockSpec(memory_space=pltpu.VMEM)
    nk = bc // rows
    slopes, colsl = pl.pallas_call(
        functools.partial(comm_kernel, C, R, rows, fl),
        out_shape=[
            jax.ShapeDtypeStruct((LANES, C, rows, fl), jnp.bfloat16),
            jax.ShapeDtypeStruct((LANES, nk, rows, fl), jnp.bfloat16),
        ],
        in_specs=[any_spec, any_spec, vmem, vmem, vmem, vmem],
        out_specs=[any_spec, any_spec],
        scratch_shapes=[
            pltpu.VMEM((C, rows, kd), jnp.bfloat16),
            pltpu.VMEM((C, rows, fc), jnp.bfloat16),
            pltpu.VMEM((LANES, C - 1, rows, fl), jnp.bfloat16),
            pltpu.VMEM((LANES, C - 1, rows, fl), jnp.bfloat16),
            pltpu.VMEM((LANES, rows, fl), jnp.bfloat16),
            pltpu.VMEM((C - 1, 8, F), jnp.float32),
            pltpu.SemaphoreType.DMA((2, C)),
            pltpu.SemaphoreType.DMA((LANES, C - 1)),
            pltpu.SemaphoreType.DMA((LANES, C - 1)),
            pltpu.SemaphoreType.DMA((LANES, C - 1)),
            pltpu.SemaphoreType.DMA((LANES, C - 1)),
            pltpu.SemaphoreType.DMA((C - 1,)),
            pltpu.SemaphoreType.DMA((C - 1,)),
            pltpu.SemaphoreType.DMA((LANES, nk)),
            pltpu.SemaphoreType.DMA((LANES, nk)),
            pltpu.SemaphoreType.DMA((LANES,)),
        ],
        compiler_params=pltpu.CompilerParams(
            collective_id=0, has_side_effects=True, vmem_limit_bytes=56 * 1024 * 1024
        ),
        name="slopes_ring",
    )(
        interaction.reshape(C, rows, kd), residual.reshape(C, rows, fc),
        commands, sel, rmask, fmask,
    )
    slopes = slopes.reshape(LANES, br, fl)
    colsl = colsl.reshape(LANES, bc, fl)
    tm = divisor(br, 256, 16)
    tn = divisor(bc, 768, 128)
    return pl.pallas_call(
        functools.partial(cov_kernel, C, R, br, bc, F, tm, tn),
        grid=(br // tm,),
        out_shape=jax.ShapeDtypeStruct((br, bc), jnp.bfloat16),
        in_specs=[
            pl.BlockSpec((LANES, tm, fl), lambda i: (0, i, 0)),
            any_spec,
            any_spec,
        ],
        out_specs=pl.BlockSpec((tm, bc), lambda i: (i, 0)),
        scratch_shapes=[
            pltpu.VMEM((bc, F), jnp.bfloat16),
            pltpu.SemaphoreType.DMA((LANES,)),
        ],
        compiler_params=pltpu.CompilerParams(
            dimension_semantics=("arbitrary",), vmem_limit_bytes=48 * 1024 * 1024
        ),
        name="covariance_upper",
    )(slopes, slopes, colsl)


def solution(mesh):
    placed = (P("row", "col"), P("row", "col"), P("col", None), P("row"), P("col"))
    return jax.shard_map(
        functools.partial(per_device, mesh.shape["row"], mesh.shape["col"]),
        mesh=mesh, in_specs=placed, out_specs=P("row", "col"), check_vma=False,
    )
```

```python
import functools

import jax
import jax.numpy as jnp
from jax import lax
from jax.experimental import pallas as pl
from jax.experimental.pallas import tpu as pltpu
from jax.sharding import PartitionSpec as P

SBLK = 128
MESH = pl.DeviceIdType.MESH
LANES = 4


def divisor(n, limit, unit):
    best = n
    for d in range(unit, min(n, limit) + 1, unit):
        if n % d == 0:
            best = d
    return best


def ring_position(c, n):
    return lax.rem(c + 1, 2) * (c // 2) + lax.rem(c, 2) * (n - 1 - c // 2)


def ring_column(p, n):
    up = 2 * p
    down = 2 * (n - 1 - p) + 1
    return jnp.where(p < n // 2, up, down)


def comm_kernel(
    C, R, rows, fl, inter_hbm, resid_hbm, cmd_ref, sv_ref, fv_ref,
    s_hbm, col_hbm,
    inter, resid, stage, recv, own, fall, sel_ref, fmask_ref,
    in_sem, rs_send, rs_recv, ag_send, ag_recv, m_send, m_recv, c_send, c_recv, own_sem,
):
    r = lax.axis_index("row")
    c = lax.axis_index("col")
    p = ring_position(c, C)
    nxt = ring_column(lax.rem(p + 1, C), C)
    prv = ring_column(lax.rem(p + C - 1, C), C)
    br = C * rows
    bc = br * R // C
    per_row = br // bc
    rc = c // per_row
    k0 = lax.rem(c, per_row) * (bc // rows)
    nk = bc // rows
    tile = divisor(rows, 256, 16)

    def chunk_of(q, row):
        if C % 2:
            return q
        return q // 2 + lax.rem(q + row, 2) * (C // 2)

    def load(q):
        k = chunk_of(q, r)
        return (
            pltpu.make_async_copy(inter_hbm.at[k], inter.at[k], in_sem.at[0, k]),
            pltpu.make_async_copy(resid_hbm.at[k], resid.at[k], in_sem.at[1, k]),
        )

    def start_load(k):
        for cp in load(k):
            cp.start()

    def wait_load(k):
        for cp in load(k):
            cp.wait()

    for i in range(1, C // 2):
        start_load(lax.rem(p + C - i, C))
        start_load(lax.rem(p + i, C))
    start_load(lax.rem(p + C // 2, C))
    start_load(p)

    barrier = pltpu.get_barrier_semaphore()
    for j in range(1, C):
        pl.semaphore_signal(
            barrier, inc=1, device_id=(r, lax.rem(c + j, C)), device_id_type=MESH
        )
    for j in range(1, R):
        pl.semaphore_signal(
            barrier, inc=1, device_id=(lax.rem(r + j, R), c), device_id_type=MESH
        )
    pl.semaphore_wait(barrier, C - 1 + R - 1)

    fc = resid.shape[2]
    F = fmask_ref.shape[1]
    frame_ids = lax.broadcasted_iota(jnp.int32, (fc, F), 1)
    own_ids = c * fc + lax.broadcasted_iota(jnp.int32, (fc, F), 0)
    sel_ref[...] = jnp.where(frame_ids == own_ids, 1.0, 0.0).astype(jnp.bfloat16)
    valid = jnp.broadcast_to(fv_ref[...].astype(jnp.float32), (8, fc))
    fmask_ref[...] = jnp.dot(
        valid.astype(jnp.bfloat16), sel_ref[...], preferred_element_type=jnp.float32
    )

    def mask_copy(j):
        return pltpu.make_async_remote_copy(
            src_ref=fmask_ref, dst_ref=fall.at[j - 1],
            send_sem=m_send.at[j - 1], recv_sem=m_recv.at[j - 1],
            device_id=(r, lax.rem(c + j, C)), device_id_type=MESH,
        )

    for j in range(1, C):
        mask_copy(j).start()

    def lane_is_up(l):
        return l < LANES // 2

    def rs_chunk(l, s):
        if lane_is_up(l):
            return chunk_of(lax.rem(p + 2 * C - 1 - s, C), r)
        return chunk_of(lax.rem(p + 1 + s, C), r)

    def ag_chunk(l, s):
        if lane_is_up(l):
            return chunk_of(lax.rem(p + 2 * C - s, C), r)
        return chunk_of(lax.rem(p + s, C), r)

    def rs_copy(l, s):
        return pltpu.make_async_remote_copy(
            src_ref=stage.at[l, s], dst_ref=recv.at[l, s],
            send_sem=rs_send.at[l, s], recv_sem=rs_recv.at[l, s],
            device_id=(r, nxt if lane_is_up(l) else prv), device_id_type=MESH,
        )

    def partial(l, k, t):
        at = pl.ds(pl.multiple_of(t * tile, 8), tile)
        cols = slice(l * fl, (l + 1) * fl)
        return jnp.dot(
            inter[k, at, :], cmd_ref[:, cols], preferred_element_type=jnp.float32
        ) + jnp.dot(
            resid[k, at, :], sel_ref[:, cols], preferred_element_type=jnp.float32
        )

    def rs_step(s, first):
        for l in range(LANES):
            k = rs_chunk(l, s)
            if not first:
                rs_copy(l, s - 1).wait_recv()

            def one(t, _, l=l, k=k):
                at = pl.ds(pl.multiple_of(t * tile, 8), tile)
                value = partial(l, k, t)
                if not first:
                    value = value + recv[l, s - 1, at, :].astype(jnp.float32)
                stage[l, s, at, :] = value.astype(jnp.bfloat16)
                return 0

            lax.fori_loop(0, rows // tile, one, 0)
            rs_copy(l, s).start()

    for s in range(C - 1):
        i = s + 1
        if i < C // 2:
            wait_load(lax.rem(p + C - i, C))
            wait_load(lax.rem(p + i, C))
        elif i == C // 2:
            wait_load(lax.rem(p + C // 2, C))
            wait_load(p)
        if s <= C // 2:
            rs_step(s, s == 0)
    if C - 1 > C // 2 + 1:
        lax.fori_loop(C // 2 + 1, C - 1, lambda s, _: (rs_step(s, False), 0)[1], 0)

    for j in range(1, C):
        mask_copy(j).wait_recv()
    frames = fmask_ref[...]
    for j in range(1, C):
        frames = frames + fall[j - 1]

    def ag_copy(l, s, from_own=False):
        k = ag_chunk(l, s)
        return pltpu.make_async_remote_copy(
            src_ref=own.at[l] if from_own else s_hbm.at[l, k],
            dst_ref=s_hbm.at[l, k],
            send_sem=ag_send.at[l, s], recv_sem=ag_recv.at[l, s],
            device_id=(r, nxt if lane_is_up(l) else prv), device_id_type=MESH,
        )

    kp = chunk_of(p, r)
    nb = sv_ref.shape[1]
    valid_rows = sv_ref[...].astype(jnp.float32)

    def own_copy(l):
        return pltpu.make_async_copy(own.at[l], s_hbm.at[l, kp], own_sem.at[l])

    for l in range(LANES):
        rs_copy(l, C - 2).wait_recv()

        def last(t, _, l=l):
            at = pl.ds(pl.multiple_of(t * tile, 8), tile)
            value = partial(l, kp, t) + recv[l, C - 2, at, :].astype(jnp.float32)
            ids = kp * rows + t * tile + lax.broadcasted_iota(jnp.int32, (tile, nb), 0)
            first = SBLK * lax.broadcasted_iota(jnp.int32, (tile, nb), 1)
            inside = (ids >= first) & (ids < first + SBLK)
            rmask = jnp.sum(jnp.where(inside, valid_rows, 0.0), axis=1, keepdims=True)
            value = value * rmask * frames[0:1, l * fl:(l + 1) * fl]
            own[l, at, :] = value.astype(jnp.bfloat16)
            return 0

        lax.fori_loop(0, rows // tile, last, 0)
        ag_copy(l, 0, True).start()
        own_copy(l).start()

    odd = lax.rem(r, 2) == 1
    chip, root_chip = r // 2, rc // 2
    child = (lax.rem(r + R - 1, R), lax.rem(chip * 2 + R - 1, R))
    sends = (
        (r <= rc) & odd,
        (r <= rc) & (chip >= 1) & (odd | (r == rc)),
    )
    lag = 2 * (root_chip - chip) + jnp.where((r < rc) & jnp.logical_not(odd), 1, 0)

    def down(b, l, k, from_slopes=False):
        return pltpu.make_async_remote_copy(
            src_ref=s_hbm.at[l, k] if from_slopes else col_hbm.at[l, k - k0],
            dst_ref=col_hbm.at[l, k - k0],
            send_sem=c_send.at[b, l, k - k0], recv_sem=c_recv.at[l, k - k0],
            device_id=(child[b], c), device_id_type=MESH,
        )

    def chain(u):
        t = u - lag
        for l in range(LANES):
            if lane_is_up(l):
                q = lax.rem(p + 4 * C * R - t, C)
            else:
                q = lax.rem(p + 4 * C * R + t, C)
            k = chunk_of(q, rc)
            live = (t >= 0) & (t < C) & (r <= rc) & (k >= k0) & (k < k0 + nk)

            @pl.when(live & (r < rc))
            def _(l=l, k=k):
                down(0, l, k).wait_recv()

            for b in range(2):
                @pl.when(live & (r < rc) & sends[b])
                def _(l=l, k=k, b=b):
                    down(b, l, k).start()

                @pl.when(live & (r == rc) & sends[b])
                def _(l=l, k=k, b=b):
                    down(b, l, k, True).start()

    for l in range(LANES):
        own_copy(l).wait()
    chain(0)

    def ag_step(s, _):
        for l in range(LANES):
            ag_copy(l, s - 1).wait_recv()
            ag_copy(l, s).start()
        chain(s)
        return 0

    lax.fori_loop(1, C - 1, ag_step, 0)
    for l in range(LANES):
        ag_copy(l, C - 2).wait_recv()

    lax.fori_loop(C - 1, C + R - 1, lambda u, _: (chain(u), 0)[1], 0)

    def drain(s, _):
        for l in range(LANES):
            rs_copy(l, s).wait_send()
            ag_copy(l, s).wait_send()
        return 0

    lax.fori_loop(0, C - 1, drain, 0)
    for j in range(1, C):
        mask_copy(j).wait_send()

    def drain_down(i, _):
        for l in range(LANES):
            for b in range(2):
                @pl.when(sends[b])
                def _(l=l, b=b):
                    down(b, l, k0 + i).wait_send()
        return 0

    lax.fori_loop(0, nk, drain_down, 0)


def cov_kernel(C, R, br, bc, F, tm, tn, rows_ref, s_hbm, col_hbm, out_ref, cols, sem):
    r = lax.axis_index("row")
    c = lax.axis_index("col")
    i = pl.program_id(0)
    per_row = br // bc
    rc = c // per_row
    fl = F // LANES

    @pl.when(i == 0)
    def _():
        def copies(src):
            return [
                pltpu.make_async_copy(
                    src(l), cols.at[:, pl.ds(l * fl, fl)], sem.at[l]
                )
                for l in range(LANES)
            ]

        start = lax.rem(c, per_row) * bc

        @pl.when(r == rc)
        def _():
            cps = copies(lambda l: s_hbm.at[l, pl.ds(pl.multiple_of(start, 8), bc), :])
            for cp in cps:
                cp.start()
            for cp in cps:
                cp.wait()

        @pl.when(r < rc)
        def _():
            cps = copies(lambda l: col_hbm.at[l])
            for cp in cps:
                cp.start()
            for cp in cps:
                cp.wait()

    row0 = r * br + i * tm
    col_base = c * bc
    spans = [(j * tn, slice(j * tn, (j + 1) * tn)) for j in range(bc // tn)]

    def value(at):
        a = jnp.concatenate([rows_ref[l] for l in range(LANES)], axis=1)
        return lax.dot_general(
            a, cols[at, :], (((1,), (1,)), ((), ())), preferred_element_type=jnp.float32
        ) / F

    above = row0 + tm <= col_base
    below = row0 >= col_base + bc

    @pl.when(above)
    def _():
        for _, at in spans:
            out_ref[:, at] = value(at).astype(jnp.bfloat16)

    @pl.when(below)
    def _():
        for _, at in spans:
            out_ref[:, at] = jnp.zeros((tm, tn), jnp.bfloat16)

    @pl.when(jnp.logical_not(above | below))
    def _():
        for off, at in spans:
            col0 = col_base + off

            @pl.when(row0 >= col0 + tn)
            def _(at=at):
                out_ref[:, at] = jnp.zeros((tm, tn), jnp.bfloat16)

            @pl.when(row0 + tm <= col0)
            def _(at=at):
                out_ref[:, at] = value(at).astype(jnp.bfloat16)

            @pl.when((row0 < col0 + tn) & (row0 + tm > col0))
            def _(at=at, col0=col0):
                rid = row0 + lax.broadcasted_iota(jnp.int32, (tm, tn), 0)
                cid = col0 + lax.broadcasted_iota(jnp.int32, (tm, tn), 1)
                out_ref[:, at] = jnp.where(rid <= cid, value(at), 0.0).astype(jnp.bfloat16)


def per_device(R, C, residual, interaction, commands, slope_valid, frame_valid):
    br, kd = interaction.shape
    F = commands.shape[1]
    fc = residual.shape[1]
    rows = br // C
    fl = F // LANES
    bc = br * R // C
    any_spec = pl.BlockSpec(memory_space=pl.ANY)
    vmem = pl.BlockSpec(memory_space=pltpu.VMEM)
    nk = bc // rows
    slopes, colsl = pl.pallas_call(
        functools.partial(comm_kernel, C, R, rows, fl),
        out_shape=[
            jax.ShapeDtypeStruct((LANES, C, rows, fl), jnp.bfloat16),
            jax.ShapeDtypeStruct((LANES, nk, rows, fl), jnp.bfloat16),
        ],
        in_specs=[any_spec, any_spec, vmem, vmem, vmem],
        out_specs=[any_spec, any_spec],
        scratch_shapes=[
            pltpu.VMEM((C, rows, kd), jnp.bfloat16),
            pltpu.VMEM((C, rows, fc), jnp.bfloat16),
            pltpu.VMEM((LANES, C - 1, rows, fl), jnp.bfloat16),
            pltpu.VMEM((LANES, C - 1, rows, fl), jnp.bfloat16),
            pltpu.VMEM((LANES, rows, fl), jnp.bfloat16),
            pltpu.VMEM((C - 1, 8, F), jnp.float32),
            pltpu.VMEM((fc, F), jnp.bfloat16),
            pltpu.VMEM((8, F), jnp.float32),
            pltpu.SemaphoreType.DMA((2, C)),
            pltpu.SemaphoreType.DMA((LANES, C - 1)),
            pltpu.SemaphoreType.DMA((LANES, C - 1)),
            pltpu.SemaphoreType.DMA((LANES, C - 1)),
            pltpu.SemaphoreType.DMA((LANES, C - 1)),
            pltpu.SemaphoreType.DMA((C - 1,)),
            pltpu.SemaphoreType.DMA((C - 1,)),
            pltpu.SemaphoreType.DMA((2, LANES, nk)),
            pltpu.SemaphoreType.DMA((LANES, nk)),
            pltpu.SemaphoreType.DMA((LANES,)),
        ],
        compiler_params=pltpu.CompilerParams(
            collective_id=0, has_side_effects=True, vmem_limit_bytes=56 * 1024 * 1024
        ),
        name="slopes_ring",
    )(
        interaction.reshape(C, rows, kd), residual.reshape(C, rows, fc),
        commands, slope_valid[None, :], frame_valid[None, :],
    )
    slopes = slopes.reshape(LANES, br, fl)
    colsl = colsl.reshape(LANES, bc, fl)
    tm = divisor(br, 768, 16)
    tn = divisor(bc, 768, 128)
    return pl.pallas_call(
        functools.partial(cov_kernel, C, R, br, bc, F, tm, tn),
        grid=(br // tm,),
        out_shape=jax.ShapeDtypeStruct((br, bc), jnp.bfloat16),
        in_specs=[
            pl.BlockSpec((LANES, tm, fl), lambda i: (0, i, 0)),
            any_spec,
            any_spec,
        ],
        out_specs=pl.BlockSpec((tm, bc), lambda i: (i, 0)),
        scratch_shapes=[
            pltpu.VMEM((bc, F), jnp.bfloat16),
            pltpu.SemaphoreType.DMA((LANES,)),
        ],
        compiler_params=pltpu.CompilerParams(
            dimension_semantics=("arbitrary",), vmem_limit_bytes=62 * 1024 * 1024
        ),
        name="covariance_upper",
    )(slopes, slopes, colsl)


def solution(mesh):
    placed = (P("row", "col"), P("row", "col"), P("col", None), P("row"), P("col"))
    return jax.shard_map(
        functools.partial(per_device, mesh.shape["row"], mesh.shape["col"]),
        mesh=mesh, in_specs=placed, out_specs=P("row", "col"), check_vma=False,
    )
```

```python
import functools

import jax
import jax.numpy as jnp
from jax import lax
from jax.experimental import pallas as pl
from jax.experimental.pallas import tpu as pltpu
from jax.sharding import PartitionSpec as P

SBLK = 128
MESH = pl.DeviceIdType.MESH
LANES = 4


def divisor(n, limit, unit):
    best = n
    for d in range(unit, min(n, limit) + 1, unit):
        if n % d == 0:
            best = d
    return best


def ring_position(c, n):
    return lax.rem(c + 1, 2) * (c // 2) + lax.rem(c, 2) * (n - 1 - c // 2)


def ring_column(p, n):
    up = 2 * p
    down = 2 * (n - 1 - p) + 1
    return jnp.where(p < n // 2, up, down)


def comm_kernel(
    C, R, rows, fl, inter_hbm, resid_hbm, cmd_ref, sv_ref, fv_ref,
    s_hbm, col_hbm,
    inter, resid_t, resid, stage, recv, own, fall, sel_ref, fmask_ref,
    in_sem, rs_send, rs_recv, ag_send, ag_recv, m_send, m_recv, c_send, c_recv, own_sem, resid_sem,
):
    r = lax.axis_index("row")
    c = lax.axis_index("col")
    p = ring_position(c, C)
    nxt = ring_column(lax.rem(p + 1, C), C)
    prv = ring_column(lax.rem(p + C - 1, C), C)
    br = C * rows
    bc = br * R // C
    per_row = br // bc
    rc = c // per_row
    k0 = lax.rem(c, per_row) * (bc // rows)
    nk = bc // rows
    tile = divisor(rows, 256, 16)

    def chunk_of(q, row):
        if C % 2:
            return q
        return q // 2 + lax.rem(q + row, 2) * (C // 2)

    def load(q):
        k = chunk_of(q, r)
        return pltpu.make_async_copy(inter_hbm.at[k], inter.at[k], in_sem.at[k])

    def start_load(k):
        load(k).start()

    def wait_load(k):
        load(k).wait()

    barrier = pltpu.get_barrier_semaphore()
    for j in range(1, C):
        pl.semaphore_signal(
            barrier, inc=1, device_id=(r, lax.rem(c + j, C)), device_id_type=MESH
        )
    for j in range(1, R):
        pl.semaphore_signal(
            barrier, inc=1, device_id=(lax.rem(r + j, R), c), device_id_type=MESH
        )
    resid_copy = pltpu.make_async_copy(resid_hbm, resid_t, resid_sem)
    resid_copy.start()
    for i in range(1, C // 2):
        start_load(lax.rem(p + C - i, C))
        start_load(lax.rem(p + i, C))
    start_load(lax.rem(p + C // 2, C))
    start_load(p)

    fc = resid.shape[1]
    F = fmask_ref.shape[1]
    frame_ids = lax.broadcasted_iota(jnp.int32, (fc, F), 1)
    own_ids = c * fc + lax.broadcasted_iota(jnp.int32, (fc, F), 0)
    sel_ref[...] = jnp.where(frame_ids == own_ids, 1.0, 0.0).astype(jnp.bfloat16)
    valid = jnp.broadcast_to(fv_ref[...].astype(jnp.float32), (8, fc))
    fmask_ref[...] = jnp.dot(
        valid.astype(jnp.bfloat16), sel_ref[...], preferred_element_type=jnp.float32
    )

    def mask_copy(j):
        return pltpu.make_async_remote_copy(
            src_ref=fmask_ref, dst_ref=fall.at[j - 1],
            send_sem=m_send.at[j - 1], recv_sem=m_recv.at[j - 1],
            device_id=(r, lax.rem(c + j, C)), device_id_type=MESH,
        )

    resid_copy.wait()
    width = divisor(br, 512, 128)

    def turn(i, _):
        at = pl.ds(pl.multiple_of(i * width, 128), width)
        resid[at, :] = resid_t[:, at].astype(jnp.float32).T
        return 0

    lax.fori_loop(0, br // width, turn, 0)

    def lane_is_up(l):
        return l % 2 == 0

    def rs_chunk(l, s):
        if lane_is_up(l):
            return chunk_of(lax.rem(p + 2 * C - 1 - s, C), r)
        return chunk_of(lax.rem(p + 1 + s, C), r)

    def ag_chunk(l, s):
        if lane_is_up(l):
            return chunk_of(lax.rem(p + 2 * C - s, C), r)
        return chunk_of(lax.rem(p + s, C), r)

    def rs_copy(l, s):
        return pltpu.make_async_remote_copy(
            src_ref=stage.at[l, s], dst_ref=recv.at[l, s],
            send_sem=rs_send.at[l, s], recv_sem=rs_recv.at[l, s],
            device_id=(r, nxt if lane_is_up(l) else prv), device_id_type=MESH,
        )

    def partial(l, k, t):
        at = pl.ds(pl.multiple_of(t * tile, 8), tile)
        cols = slice(l * fl, (l + 1) * fl)
        return jnp.dot(
            inter[k, at, :], cmd_ref[:, cols], preferred_element_type=jnp.float32
        ) + jnp.dot(
            resid[pl.ds(pl.multiple_of(k * rows + t * tile, 8), tile), :].astype(jnp.bfloat16),
            sel_ref[:, cols],
            preferred_element_type=jnp.float32
        )

    def rs_step(s, first):
        for l in range(LANES):
            k = rs_chunk(l, s)
            if not first:
                rs_copy(l, s - 1).wait_recv()

            def one(t, _, l=l, k=k):
                at = pl.ds(pl.multiple_of(t * tile, 8), tile)
                value = partial(l, k, t)
                if not first:
                    value = value + recv[l, s - 1, at, :].astype(jnp.float32)
                stage[l, s, at, :] = value.astype(jnp.bfloat16)
                return 0

            lax.fori_loop(0, rows // tile, one, 0)
            if not first:
                rs_copy(l, s).start()
        if first:
            pl.semaphore_wait(barrier, C - 1 + R - 1)
            for l in range(LANES):
                rs_copy(l, s).start()
            for j in range(1, C):
                mask_copy(j).start()

    for s in range(C - 1):
        i = s + 1
        if i < C // 2:
            wait_load(lax.rem(p + C - i, C))
            wait_load(lax.rem(p + i, C))
        elif i == C // 2:
            wait_load(lax.rem(p + C // 2, C))
            wait_load(p)
        if s <= C // 2:
            rs_step(s, s == 0)
    if C - 1 > C // 2 + 1:
        lax.fori_loop(C // 2 + 1, C - 1, lambda s, _: (rs_step(s, False), 0)[1], 0)

    for j in range(1, C):
        mask_copy(j).wait_recv()
    frames = fmask_ref[...]
    for j in range(1, C):
        frames = frames + fall[j - 1]

    def ag_copy(l, s, from_own=False):
        k = ag_chunk(l, s)
        return pltpu.make_async_remote_copy(
            src_ref=own.at[l] if from_own else s_hbm.at[l, k],
            dst_ref=s_hbm.at[l, k],
            send_sem=ag_send.at[l, s], recv_sem=ag_recv.at[l, s],
            device_id=(r, nxt if lane_is_up(l) else prv), device_id_type=MESH,
        )

    kp = chunk_of(p, r)
    nb = sv_ref.shape[1]
    valid_rows = sv_ref[...].astype(jnp.float32)

    def own_copy(l):
        return pltpu.make_async_copy(own.at[l], s_hbm.at[l, kp], own_sem.at[l])

    for l in range(LANES):
        rs_copy(l, C - 2).wait_recv()

        def last(t, _, l=l):
            at = pl.ds(pl.multiple_of(t * tile, 8), tile)
            value = partial(l, kp, t) + recv[l, C - 2, at, :].astype(jnp.float32)
            ids = kp * rows + t * tile + lax.broadcasted_iota(jnp.int32, (tile, nb), 0)
            first = SBLK * lax.broadcasted_iota(jnp.int32, (tile, nb), 1)
            inside = (ids >= first) & (ids < first + SBLK)
            rmask = jnp.sum(jnp.where(inside, valid_rows, 0.0), axis=1, keepdims=True)
            value = value * rmask * frames[0:1, l * fl:(l + 1) * fl]
            own[l, at, :] = value.astype(jnp.bfloat16)
            return 0

        lax.fori_loop(0, rows // tile, last, 0)
        ag_copy(l, 0, True).start()
        own_copy(l).start()

    odd = lax.rem(r, 2) == 1
    main = lax.rem(r, 2) == lax.rem(rc, 2)
    chip, root_chip = r // 2, rc // 2
    child = (chip * 2 + 1 - lax.rem(r, 2), lax.rem(r + R - 2, R))
    sends = (
        main & ((r < rc) | ((r == rc) & odd)),
        main & (r <= rc) & (chip >= 1),
    )
    lag = 2 * (root_chip - chip) + jnp.where(main, 0, 1)

    def down(b, l, k, from_slopes=False):
        return pltpu.make_async_remote_copy(
            src_ref=s_hbm.at[l, k] if from_slopes else col_hbm.at[l, k - k0],
            dst_ref=col_hbm.at[l, k - k0],
            send_sem=c_send.at[b, l, k - k0], recv_sem=c_recv.at[l, k - k0],
            device_id=(child[b], c), device_id_type=MESH,
        )

    def chain(u):
        t = u - lag
        for l in range(LANES):
            if lane_is_up(l):
                q = lax.rem(p + 4 * C * R - t, C)
            else:
                q = lax.rem(p + 4 * C * R + t, C)
            k = chunk_of(q, rc)
            live = (t >= 0) & (t < C) & (r <= rc) & (k >= k0) & (k < k0 + nk)

            @pl.when(live & (r < rc))
            def _(l=l, k=k):
                down(0, l, k).wait_recv()

            for b in range(2):
                @pl.when(live & (r < rc) & sends[b])
                def _(l=l, k=k, b=b):
                    down(b, l, k).start()

                @pl.when(live & (r == rc) & sends[b])
                def _(l=l, k=k, b=b):
                    down(b, l, k, True).start()

    for l in range(LANES):
        own_copy(l).wait()
    chain(0)

    def ag_step(s, _):
        for l in range(LANES):
            ag_copy(l, s - 1).wait_recv()
            ag_copy(l, s).start()
        chain(s)
        return 0

    lax.fori_loop(1, C - 1, ag_step, 0)
    for l in range(LANES):
        ag_copy(l, C - 2).wait_recv()

    lax.fori_loop(C - 1, C + R - 1, lambda u, _: (chain(u), 0)[1], 0)

    def drain(s, _):
        for l in range(LANES):
            rs_copy(l, s).wait_send()
            ag_copy(l, s).wait_send()
        return 0

    lax.fori_loop(0, C - 1, drain, 0)
    for j in range(1, C):
        mask_copy(j).wait_send()

    def drain_down(i, _):
        for l in range(LANES):
            for b in range(2):
                @pl.when(sends[b])
                def _(l=l, b=b):
                    down(b, l, k0 + i).wait_send()
        return 0

    lax.fori_loop(0, nk, drain_down, 0)


def cov_kernel(C, R, br, bc, F, tm, tn, rows_ref, s_hbm, col_hbm, out_ref, cols, sem):
    r = lax.axis_index("row")
    c = lax.axis_index("col")
    i = pl.program_id(0)
    per_row = br // bc
    rc = c // per_row
    fl = F // LANES

    @pl.when(i == 0)
    def _():
        def copies(src):
            return [
                pltpu.make_async_copy(
                    src(l), cols.at[:, pl.ds(l * fl, fl)], sem.at[l]
                )
                for l in range(LANES)
            ]

        start = lax.rem(c, per_row) * bc

        @pl.when(r == rc)
        def _():
            cps = copies(lambda l: s_hbm.at[l, pl.ds(pl.multiple_of(start, 8), bc), :])
            for cp in cps:
                cp.start()
            for cp in cps:
                cp.wait()

        @pl.when(r < rc)
        def _():
            cps = copies(lambda l: col_hbm.at[l])
            for cp in cps:
                cp.start()
            for cp in cps:
                cp.wait()

    row0 = r * br + i * tm
    col_base = c * bc
    spans = [(j * tn, slice(j * tn, (j + 1) * tn)) for j in range(bc // tn)]

    def value(at):
        a = jnp.concatenate([rows_ref[l] for l in range(LANES)], axis=1)
        return lax.dot_general(
            a, cols[at, :], (((1,), (1,)), ((), ())), preferred_element_type=jnp.float32
        ) / F

    above = row0 + tm <= col_base
    below = row0 >= col_base + bc

    @pl.when(above)
    def _():
        for _, at in spans:
            out_ref[:, at] = value(at).astype(jnp.bfloat16)

    @pl.when(below)
    def _():
        for _, at in spans:
            out_ref[:, at] = jnp.zeros((tm, tn), jnp.bfloat16)

    @pl.when(jnp.logical_not(above | below))
    def _():
        for off, at in spans:
            col0 = col_base + off

            @pl.when(row0 >= col0 + tn)
            def _(at=at):
                out_ref[:, at] = jnp.zeros((tm, tn), jnp.bfloat16)

            @pl.when(row0 + tm <= col0)
            def _(at=at):
                out_ref[:, at] = value(at).astype(jnp.bfloat16)

            @pl.when((row0 < col0 + tn) & (row0 + tm > col0))
            def _(at=at, col0=col0):
                rid = row0 + lax.broadcasted_iota(jnp.int32, (tm, tn), 0)
                cid = col0 + lax.broadcasted_iota(jnp.int32, (tm, tn), 1)
                out_ref[:, at] = jnp.where(rid <= cid, value(at), 0.0).astype(jnp.bfloat16)


def per_device(R, C, residual, interaction, commands, slope_valid, frame_valid):
    br, kd = interaction.shape
    F = commands.shape[1]
    fc = residual.shape[1]
    rows = br // C
    fl = F // LANES
    bc = br * R // C
    any_spec = pl.BlockSpec(memory_space=pl.ANY)
    vmem = pl.BlockSpec(memory_space=pltpu.VMEM)
    nk = bc // rows
    slopes, colsl = pl.pallas_call(
        functools.partial(comm_kernel, C, R, rows, fl),
        out_shape=[
            jax.ShapeDtypeStruct((LANES, C, rows, fl), jnp.bfloat16),
            jax.ShapeDtypeStruct((LANES, nk, rows, fl), jnp.bfloat16),
        ],
        in_specs=[any_spec, any_spec, vmem, vmem, vmem],
        out_specs=[any_spec, any_spec],
        scratch_shapes=[
            pltpu.VMEM((C, rows, kd), jnp.bfloat16),
            pltpu.VMEM((fc, br), jnp.bfloat16),
            pltpu.VMEM((br, fc), jnp.float32),
            pltpu.VMEM((LANES, C - 1, rows, fl), jnp.bfloat16),
            pltpu.VMEM((LANES, C - 1, rows, fl), jnp.bfloat16),
            pltpu.VMEM((LANES, rows, fl), jnp.bfloat16),
            pltpu.VMEM((C - 1, 8, F), jnp.float32),
            pltpu.VMEM((fc, F), jnp.bfloat16),
            pltpu.VMEM((8, F), jnp.float32),
            pltpu.SemaphoreType.DMA((C,)),
            pltpu.SemaphoreType.DMA((LANES, C - 1)),
            pltpu.SemaphoreType.DMA((LANES, C - 1)),
            pltpu.SemaphoreType.DMA((LANES, C - 1)),
            pltpu.SemaphoreType.DMA((LANES, C - 1)),
            pltpu.SemaphoreType.DMA((C - 1,)),
            pltpu.SemaphoreType.DMA((C - 1,)),
            pltpu.SemaphoreType.DMA((2, LANES, nk)),
            pltpu.SemaphoreType.DMA((LANES, nk)),
            pltpu.SemaphoreType.DMA((LANES,)),
            pltpu.SemaphoreType.DMA,
        ],
        compiler_params=pltpu.CompilerParams(
            collective_id=0, has_side_effects=True, vmem_limit_bytes=56 * 1024 * 1024
        ),
        name="slopes_ring",
    )(
        interaction.reshape(C, rows, kd), residual.T,
        commands, slope_valid[None, :], frame_valid[None, :],
    )
    slopes = slopes.reshape(LANES, br, fl)
    colsl = colsl.reshape(LANES, bc, fl)
    tm = divisor(br, 768, 16)
    tn = divisor(bc, 768, 128)
    return pl.pallas_call(
        functools.partial(cov_kernel, C, R, br, bc, F, tm, tn),
        grid=(br // tm,),
        out_shape=jax.ShapeDtypeStruct((br, bc), jnp.bfloat16),
        in_specs=[
            pl.BlockSpec((LANES, tm, fl), lambda i: (0, i, 0)),
            any_spec,
            any_spec,
        ],
        out_specs=pl.BlockSpec((tm, bc), lambda i: (i, 0)),
        scratch_shapes=[
            pltpu.VMEM((bc, F), jnp.bfloat16),
            pltpu.SemaphoreType.DMA((LANES,)),
        ],
        compiler_params=pltpu.CompilerParams(
            dimension_semantics=("arbitrary",), vmem_limit_bytes=62 * 1024 * 1024
        ),
        name="covariance_upper",
    )(slopes, slopes, colsl)


def solution(mesh):
    placed = (P("row", "col"), P("row", "col"), P("col", None), P("row"), P("col"))
    return jax.shard_map(
        functools.partial(per_device, mesh.shape["row"], mesh.shape["col"]),
        mesh=mesh, in_specs=placed, out_specs=P("row", "col"), check_vma=False,
    )
```
